32 devices in a mesh: gx: 16 (over z, x, core), gy: 2 (over y).
Axes of the slice: x: 2, y: 2, z: 4, core: 2. Of those that a mesh axis runs over, the one named last changes fastest.
Arguments:
- particles: float32 [64, 2, 64, 1024], P(None, None, 'gx', 'gy'), may hold values from -32 to 32, as said below
- background: float32 [2, 64, 1024], P(None, 'gx', 'gy'), may hold values from -6 to 6
- obs_tile: int32 [16, 256], P('gx', 'gy'), may hold values from 0 to 127
- obs_mask: int32 [16, 16, 256], P(None, 'gx', 'gy'), may hold values 0 or 1
- obs_value: float32 [16, 256], P('gx', 'gy'), may hold values from -6 to 6
- obs_var: float32 [16, 256], P('gx', 'gy'), may hold values from 0.1 to 1
Outputs:
- analysis: float32 [64, 2, 64, 1024], P(None, None, 'gx', 'gy')
The draws below stay inside these ranges and needn't reach their ends.
Inputs may be any that keep to these rules, and one draw needn't show every extreme that they name: `particles`: each particle is a field of order one to a few. `obs_tile`: an observation's value names tile row t // 128 and tile column t % (128) of its slab.
All inputs are finite; a program needn't handle non-finite values. No bound on the sum of `obs_mask` on one device may be relied on, other than what follows from the above.
Results may differ from the reference program's by a relative error of at most 0.0001.
Values sent between devices are 32-bit elements; how exact they have to be, the bound alone decides.
A program may use at most 64 MiB of HBM per device.

```python
import math
import jax
import jax.numpy as jnp
from jax import lax

NP = 64
LAYERS = 2
STEPS = 2
TILE = 4
CX = 4
CY = 512
OBS_DEV = 128
NX = 64
NY = 1024
TILES_DEV = 128
N_GX = 16
N_GY = 2


def draw_particles(key, part):
    keys = jax.random.split(jax.random.fold_in(key, 11), 3)
    shape = (NP, LAYERS, NX, NY)
    spread = jnp.exp(jax.random.uniform(keys[0], (NP, 1, 1, 1), jnp.float32, math.log(0.5), math.log(2.0)))
    rough = jnp.exp(jax.random.uniform(keys[1], shape, jnp.float32, math.log(0.5), math.log(1.5)))
    position = jnp.arange(NX, dtype=jnp.float32)[None, None, :, None] / NX
    noise = jnp.clip(jax.random.normal(keys[2], shape, jnp.float32), -4.0, 4.0)
    ramp = jnp.exp(math.log(3.0) * position) / math.sqrt(3.0)
    return spread * ramp * rough * noise


def touch_ends(entries, stream_key, low, top_value):
    longest = entries.shape.index(max(entries.shape))
    spots = []
    for shift in (0, 1):
        where = [jax.random.randint(jax.random.fold_in(stream_key, axis), (), 0, length) for axis, length in enumerate(entries.shape)]
        where[longest] = (where[longest] + shift) % entries.shape[longest]
        spots.append(tuple(where))
    return entries.at[spots[0]].set(low).at[spots[1]].set(top_value)


def block_levels(key, dims, shards, smallest, top_value):
    gain, own = 1.0, jax.random.fold_in(key, 6)
    for dim, parts in shards:
        steps = jnp.exp(jax.random.uniform(jax.random.fold_in(own, dim), (parts,), jnp.float32, smallest / len(shards), top_value / len(shards)))
        gain = gain * jnp.repeat(steps, dims[dim] // parts).reshape([-1 if axis == dim else 1 for axis in range(len(dims))])
    return gain


def bell_draw(key, shape, scale, most, shards=(), held_as=jnp.bfloat16):
    result = scale * jax.random.normal(key, shape, jnp.float32)
    if shards:
        result = result * block_levels(key, shape, shards, -0.22, 0.18)
    return jnp.clip(result, -most, most).astype(held_as)


def setup_inputs(seed: int = 0) -> dict:
    streams_of = jax.random.split(jax.random.key(seed), 7)
    return {
        "particles": draw_particles(jax.random.fold_in(streams_of[6], 71), 0),
        "background": bell_draw(streams_of[1], (LAYERS, NX, NY), 1.0, 6.0, ((1, 16), (2, 2)), jnp.float32),
        "obs_tile": touch_ends(jax.random.randint(streams_of[2], (N_GX, N_GY * OBS_DEV), 0, TILES_DEV), jax.random.fold_in(streams_of[2], 1), 0, TILES_DEV - 1).astype(jnp.int32),
        "obs_mask": touch_ends((jax.random.randint(streams_of[3], (TILE * TILE, N_GX, N_GY * OBS_DEV), 0, 2) < 1).astype(jnp.int32), jax.random.fold_in(streams_of[3], 1), 0, 1),
        "obs_value": bell_draw(streams_of[4], (N_GX, N_GY * OBS_DEV), 1.0, 6.0, ((0, 16), (1, 2)), jnp.float32),
        "obs_var": jnp.clip(jnp.exp(math.log(1.0) - 2.3025851 * jax.random.uniform(streams_of[5], (N_GX, N_GY * OBS_DEV), jnp.float32) ** block_levels(streams_of[5], (N_GX, N_GY * OBS_DEV), ((0, 16), (1, 2)), -0.2, 0.2)), 0.1, 1.0),
    }


lap_weight = 0.25
prior_weight = 0.05
couple_weight = 0.5
step_length = 1.0
epsilon = 1e-06
highest = lax.Precision.HIGHEST

def laplace(field):
    total = jnp.roll(field, -1, -1) + jnp.roll(field, 1, -1)
    total = total + jnp.roll(field, -1, -2) + jnp.roll(field, 1, -2)
    return total - 4.0 * field

def prior_one(deviation):
    smooth = deviation - lap_weight * laplace(deviation)
    curved = smooth - lap_weight * laplace(smooth)
    return -prior_weight * (curved + couple_weight * (deviation - deviation[::-1]))

def reference(particles, background, obs_tile, obs_mask, obs_value, obs_var):
    tile_cols = CY // TILE
    block = jnp.arange(N_GX, dtype=jnp.int32)[:, None]
    column = jnp.arange(N_GY * OBS_DEV, dtype=jnp.int32)[None, :]
    offset = jnp.arange(TILE * TILE, dtype=jnp.int32)[:, None, None]
    rows = block * CX + obs_tile // tile_cols * TILE + offset // TILE
    cols = column // OBS_DEV * CY + obs_tile % tile_cols * TILE + offset % TILE
    weights = obs_mask.astype(jnp.float32)
    total_size = float(LAYERS * NX * NY)
    pair_count = float(NP * (NP - 1))
    off_diag = 1.0 - jnp.eye(NP, dtype=jnp.float32)
    state = particles
    for step in range(STEPS):
        deviation = state - background[None]
        prior_term = lax.map(prior_one, deviation)
        upper = state[:, 0]
        values = upper[:, rows, cols]
        mapped = 0.25 * lax.optimization_barrier(jnp.sum(weights[None] * values, axis=1))
        innovation = (obs_value[None] - mapped) / obs_var[None]
        contrib = (0.25 * weights)[None] * innovation[:, None]
        obs_upper = jnp.zeros((NP, NX, NY), jnp.float32).at[:, rows, cols].add(contrib)
        obs_term = jnp.stack([obs_upper, jnp.zeros_like(obs_upper)], axis=1)
        gradient = prior_term + obs_term
        flat_dev = deviation.reshape(NP, -1)
        flat_grad = gradient.reshape(NP, -1)
        gram = jnp.dot(flat_dev, flat_dev.T, precision=highest)
        diagonal = jnp.diagonal(gram)
        distance = diagonal[:, None] + diagonal[None, :] - 2.0 * gram
        width = jnp.sum(distance * off_diag) / (pair_count * total_size) + epsilon
        kernel = jnp.exp(-distance / (2.0 * width * total_size))
        attract = jnp.dot(kernel, flat_grad, precision=highest)
        pulled = jnp.dot(kernel, flat_dev, precision=highest)
        drift = (attract + (lax.optimization_barrier(jnp.sum(kernel, axis=1))[:, None] * flat_dev - pulled) / width) / NP
        scale = step_length / jnp.sqrt(jnp.sum(drift * drift) / (NP * total_size) + epsilon)
        state = state + scale * drift.reshape(state.shape)
    return state
```

```python
import functools

import jax
import jax.numpy as jnp
from jax import lax
from jax.experimental import pallas as pl
from jax.experimental.pallas import tpu as pltpu
from jax.sharding import PartitionSpec as P

TILE = 4
CHUNK = 16
LANES = 128
lap_weight = 0.25
prior_weight = 0.05
couple_weight = 0.5
step_length = 1.0
epsilon = 1e-06
highest = lax.Precision.HIGHEST
MESH = pl.DeviceIdType.MESH
F32 = jnp.float32
BF16 = jnp.bfloat16


def split(x):
    high = x.astype(BF16)
    return high, (x - high.astype(F32)).astype(BF16)


def dot_nn(a, b, precision=None):
    return lax.dot_general(
        a, b, (((1,), (0,)), ((), ())), precision=precision, preferred_element_type=F32
    )


def dot_nt(a, b, precision=None):
    return lax.dot_general(
        a, b, (((1,), (1,)), ((), ())), precision=precision, preferred_element_type=F32
    )


def total(x):
    return jnp.sum(jnp.sum(x, axis=1, keepdims=True), axis=0, keepdims=True)


def kernel(
    n_gx, n_gy, size,
    state, background, tile, mask, values, variance,
    out,
    fld, hf, xl, xh, yp, yr, dl, dh, hmat, gpart, grecv, gres, gsum, spart, srecv, small,
    send, recv, gsend, grsem, asend, arsem, ssend, srsem,
):
    layers, rows, count, cols = state.shape
    chunks = count // CHUNK
    n_dev = n_gx * n_gy
    gx = lax.axis_index("gx")
    gy = lax.axis_index("gy")
    up = lax.rem(gx + 1, n_gx)
    down = lax.rem(gx + n_gx - 1, n_gx)
    side = lax.rem(gy + 1, n_gy)
    me = gx * n_gy + gy

    def device(offset):
        other = lax.rem(me + offset, n_dev)
        return other, (lax.div(other, n_gy), lax.rem(other, n_gy))

    barrier = pltpu.get_barrier_semaphore()

    def greet(offset, carry):
        pl.semaphore_signal(barrier, inc=1, device_id=device(offset)[1], device_id_type=MESH)
        return carry

    lax.fori_loop(1, n_dev, greet, 0)

    lane = lax.broadcasted_iota(jnp.int32, (CHUNK, LANES), 1)

    def pack(f, l, r, ps):
        yp[f, l, r, ps, :] = jnp.where(
            lane < LANES // 2,
            fld[f, l, r, ps, pl.ds(0, LANES)],
            fld[f, l, r, ps, pl.ds(cols - LANES, LANES)],
        )

    def copies(f, c):
        ps = pl.ds(pl.multiple_of(c * CHUNK, CHUNK), CHUNK)
        pairs = (
            (fld.at[f, :, pl.ds(rows - 2, 2), ps, :], xl.at[f, :, :, ps, :], (up, gy)),
            (fld.at[f, :, pl.ds(0, 2), ps, :], xh.at[f, :, :, ps, :], (down, gy)),
            (yp.at[f, :, :, ps, :], yr.at[f, :, :, ps, :], (gx, side)),
            (yp.at[f, :, rows - 1, ps, :], dl.at[f, :, ps, :], (up, side)),
            (yp.at[f, :, 0, ps, :], dh.at[f, :, ps, :], (down, side)),
        )
        return [
            pltpu.make_async_remote_copy(
                src_ref=source,
                dst_ref=target,
                send_sem=send.at[f, kind, c],
                recv_sem=recv.at[f, kind, c],
                device_id=where,
                device_id_type=MESH,
            )
            for kind, (source, target, where) in enumerate(pairs)
        ]

    def prior(f, c, emit):
        ps = pl.ds(pl.multiple_of(c * CHUNK, CHUNK), CHUNK)
        for r in range(rows):
            for l in range(layers):
                def row(k):
                    if k < 0:
                        return xl[f, l, k + 2, ps, :]
                    if k >= rows:
                        return xh[f, l, k - rows, ps, :]
                    return fld[f, l, k, ps, :]

                def edge(k):
                    if k < 0:
                        return dl[f, l, ps, :]
                    if k >= rows:
                        return dh[f, l, ps, :]
                    return yr[f, l, k, ps, :]

                here = row(r)
                near = row(r - 1) + row(r + 1)
                far = row(r - 2) + row(r + 2)
                wide = 0.125 * near - here
                edge_here = edge(r)
                edge_wide = 0.125 * (edge(r - 1) + edge(r + 1)) - edge_here

                def shifted(x, e, by):
                    left = pltpu.roll(x, by, 1)
                    first = jnp.where(lane < by, pltpu.roll(e, by, 1), left[:, :LANES])
                    left = jnp.concatenate([first, left[:, LANES:]], axis=1)
                    right = pltpu.roll(x, cols - by, 1)
                    last = jnp.where(
                        lane >= LANES - by, pltpu.roll(e, LANES - by, 1), right[:, cols - LANES :]
                    )
                    right = jnp.concatenate([right[:, : cols - LANES], last], axis=1)
                    return left + right

                curved = 4.25 * here - near + 0.0625 * (far + shifted(here, edge_here, 2))
                curved = curved + shifted(wide, edge_wide, 1)
                other = fld[f, 1 - l, r, ps, :]
                emit(l, r, ps, -prior_weight * (curved + couple_weight * (here - other)))

    def begin(c, carry):
        ps = pl.ds(pl.multiple_of(c * CHUNK, CHUNK), CHUNK)
        for l in range(layers):
            for r in range(rows):
                fld[0, l, r, ps, :] = state[l, r, ps, :] - background[l, pl.ds(r, 1), :]
                pack(0, l, r, ps)
        return carry

    lax.fori_loop(0, chunks, begin, 0)
    pl.semaphore_wait(barrier, n_dev - 1)

    def send_first(c, carry):
        for copy in copies(0, c):
            copy.start()
        return carry

    lax.fori_loop(0, chunks, send_first, 0)

    n_obs = tile.shape[1]
    column = lax.broadcasted_iota(jnp.int32, (cols, n_obs), 0)
    hit = lax.div(column, TILE) == tile[...]
    for r in range(rows):
        weights = 0.25 * mask[pl.ds(r * TILE, TILE), :].astype(F32)
        weights = jnp.concatenate([weights, weights], axis=0)
        weights = jnp.concatenate([weights] * (cols // (2 * TILE)), axis=0)
        hmat[r] = jnp.where(hit, weights, 0.0).astype(BF16)

    def mapped_of(upper):
        acc = jnp.zeros((2 * count, n_obs), F32)
        for r in range(rows):
            acc = acc + dot_nn(jnp.concatenate(split(upper(r)), axis=0), hmat[r])
        return acc[:count] + acc[count:]

    def spread_of(innovation, emit):
        both = jnp.concatenate(split(innovation), axis=0)
        for r in range(rows):
            back = dot_nt(both, hmat[r])
            emit(r, back[:count] + back[count:])

    def put_obs(r, x):
        hf[0, r] = x

    mapped = mapped_of(lambda r: state[0, r])
    spread_of((values[...] - mapped) / variance[...], put_obs)

    def gradient(c, carry):
        for copy in copies(0, c):
            copy.wait_recv()

        def emit(l, r, ps, x):
            fld[1, l, r, ps, :] = x + hf[0, r, ps, :] if l == 0 else x
            pack(1, l, r, ps)

        prior(0, c, emit)
        for copy in copies(1, c):
            copy.start()
        return carry

    lax.fori_loop(0, chunks, gradient, 0)

    same = jnp.zeros((2 * count, 2 * count), F32)
    cross = jnp.zeros((2 * count, 2 * count), F32)
    for l in range(layers):
        for r in range(rows):
            high, low = split(jnp.concatenate([fld[0, l, r], fld[1, l, r]], axis=0))
            same = same + dot_nt(high, high)
            cross = cross + dot_nt(high, low)
    gram = same + cross + cross.T
    share = gpart.shape[1]
    owners = 2 * count // share
    for o in range(owners):
        gpart[o] = gram[o * share : (o + 1) * share]
    if owners < n_dev:
        gpart[pl.ds(owners, n_dev - owners)] = jnp.zeros((n_dev - owners, share, 2 * count), F32)

    def scatter(k):
        other, where = device(k)
        return pltpu.make_async_remote_copy(
            src_ref=gpart.at[other], dst_ref=grecv.at[k], send_sem=gsend.at[k],
            recv_sem=grsem.at[k], device_id=where, device_id_type=MESH,
        )

    def gather(k):
        other, where = device(k)
        return pltpu.make_async_remote_copy(
            src_ref=gsum, dst_ref=gres.at[me], send_sem=asend.at[k],
            recv_sem=arsem.at[k], device_id=where, device_id_type=MESH,
        )

    def share_out(k):
        other, where = device(k)
        return pltpu.make_async_remote_copy(
            src_ref=spart, dst_ref=srecv.at[k], send_sem=ssend.at[k],
            recv_sem=srsem.at[k], device_id=where, device_id_type=MESH,
        )

    def each(make, act):
        def step(k, carry):
            act(make(k))
            return carry

        lax.fori_loop(1, n_dev, step, 0)

    each(scatter, lambda copy: copy.start())

    mapped = mapped_of(lambda r: fld[1, 0, r])
    spread_of(-mapped / variance[...], put_obs)

    grecv[0] = gpart[me]
    each(scatter, lambda copy: copy.wait_recv())
    gsum[...] = jnp.sum(grecv[...], axis=0)
    gres[me] = gsum[...]
    each(gather, lambda copy: copy.start())

    def second(c, carry):
        for copy in copies(1, c):
            copy.wait_recv()

        def emit(l, r, ps, x):
            hf[l, r, ps, :] = x + hf[0, r, ps, :] if l == 0 else x

        prior(1, c, emit)
        return carry

    lax.fori_loop(0, chunks, second, 0)

    each(gather, lambda copy: copy.wait_recv())
    gram = jnp.concatenate([gres[o] for o in range(owners)], axis=0)
    eye = (
        lax.broadcasted_iota(jnp.int32, (count, count), 0)
        == lax.broadcasted_iota(jnp.int32, (count, count), 1)
    ).astype(F32)

    def mixing(matrix):
        diagonal = matrix * eye
        distance = (
            jnp.sum(diagonal, axis=1, keepdims=True)
            + jnp.sum(diagonal, axis=0, keepdims=True)
            - 2.0 * matrix
        )
        width = total(distance * (1.0 - eye)) / (count * (count - 1.0) * size) + epsilon
        weight = jnp.exp(-distance / (2.0 * width * size))
        pull = (jnp.sum(weight, axis=1, keepdims=True) * eye - weight) / (width * count)
        return weight / count, pull

    dev_gram = gram[:count, :count]
    attract, pull = mixing(dev_gram)
    small[0] = jnp.concatenate([pull, attract], axis=1)
    weights = small[0]
    small[1] = dot_nn(weights, gram, highest)
    partial = small[1]
    square = dot_nt(partial, weights, highest)
    crossed = dot_nt(gram[:count], weights, highest)
    small[2] = jnp.concatenate([square, crossed], axis=1)
    square = small[2, :, pl.ds(0, count)]
    crossed = small[2, :, pl.ds(count, count)]
    scale = step_length / jnp.sqrt(total(square * eye) / (count * size) + epsilon)
    next_gram = dev_gram + scale * (crossed + partial[:, :count]) + scale * scale * square
    attract_next, pull_next = mixing(next_gram)
    products = scale * dot_nn(jnp.concatenate([attract_next, pull_next], axis=0), weights, highest)
    on_dev = pull_next + products[count:, :count]
    on_grad = attract_next + products[:count, :count] + products[count:, count:]
    on_second = products[:count, count:]
    zero = jnp.zeros((count, count), F32)
    left = jnp.concatenate(
        [
            jnp.concatenate([on_dev, on_grad, on_second], axis=1),
            jnp.concatenate([scale * pull, scale * attract, zero], axis=1),
        ],
        axis=0,
    )
    left_high, left_low = split(left)
    left_both = jnp.concatenate([left_high, left_low], axis=0)
    sums = jnp.zeros((count, cols), F32)
    for l in range(layers):
        for r in range(rows):
            high, low = split(jnp.concatenate([fld[0, l, r], fld[1, l, r], hf[l, r]], axis=0))
            main = dot_nn(left_both, high)
            mixed = main[: 2 * count] + main[2 * count :] + dot_nn(left_high, low)
            drift = mixed[:count]
            hf[l, r] = drift
            out[l, r] = state[l, r] + mixed[count:]
            sums = sums + drift * drift
    sums = jnp.sum(sums, axis=0, keepdims=True)
    folded = sums[:, :LANES]
    for k in range(1, cols // LANES):
        folded = folded + sums[:, k * LANES : (k + 1) * LANES]
    spart[...] = folded
    srecv[0] = folded
    each(share_out, lambda copy: copy.start())
    each(share_out, lambda copy: copy.wait_recv())
    whole = total(jnp.sum(srecv[...], axis=0))
    scale_next = step_length / jnp.sqrt(whole / (count * size) + epsilon)
    for l in range(layers):
        for r in range(rows):
            out[l, r] = out[l, r] + scale_next * hf[l, r]

    def drain(c, carry):
        for f in range(2):
            for copy in copies(f, c):
                copy.wait_send()
        return carry

    lax.fori_loop(0, chunks, drain, 0)
    each(scatter, lambda copy: copy.wait_send())
    each(gather, lambda copy: copy.wait_send())
    each(share_out, lambda copy: copy.wait_send())


def per_device(n_gx, n_gy, particles, background, obs_tile, obs_mask, obs_value, obs_var):
    count, layers, rows, cols = particles.shape
    assert rows == TILE and n_gy == 2 and count % CHUNK == 0
    n_dev = n_gx * n_gy
    size = float(layers * rows * cols * n_dev)
    n_obs = obs_tile.shape[1]
    share = max(1, 2 * count // n_dev)
    chunks = count // CHUNK
    dma = pltpu.SemaphoreType.DMA
    planes = particles.transpose(1, 2, 0, 3)
    vmem = pl.BlockSpec(memory_space=pltpu.VMEM)
    result = pl.pallas_call(
        functools.partial(kernel, n_gx, n_gy, size),
        out_shape=jax.ShapeDtypeStruct((layers, rows, count, cols), F32),
        in_specs=[vmem] * 6,
        out_specs=vmem,
        scratch_shapes=[
            pltpu.VMEM((2, layers, rows, count, cols), F32),
            pltpu.VMEM((layers, rows, count, cols), F32),
            pltpu.VMEM((2, layers, 2, count, cols), F32),
            pltpu.VMEM((2, layers, 2, count, cols), F32),
            pltpu.VMEM((2, layers, rows, count, LANES), F32),
            pltpu.VMEM((2, layers, rows, count, LANES), F32),
            pltpu.VMEM((2, layers, count, LANES), F32),
            pltpu.VMEM((2, layers, count, LANES), F32),
            pltpu.VMEM((rows, cols, n_obs), BF16),
            pltpu.VMEM((n_dev, share, 2 * count), F32),
            pltpu.VMEM((n_dev, share, 2 * count), F32),
            pltpu.VMEM((n_dev, share, 2 * count), F32),
            pltpu.VMEM((share, 2 * count), F32),
            pltpu.VMEM((1, LANES), F32),
            pltpu.VMEM((n_dev, 1, LANES), F32),
            pltpu.VMEM((3, count, 2 * count), F32),
            dma((2, 5, chunks)),
            dma((2, 5, chunks)),
        ]
        + [dma((n_dev,))] * 6,
        compiler_params=pltpu.CompilerParams(
            collective_id=0, has_side_effects=True, vmem_limit_bytes=48 * 2**20
        ),
    )(planes, background, obs_tile, obs_mask[:, 0], obs_value, obs_var)
    return result.transpose(2, 0, 1, 3)


def solution(mesh):
    n_gx, n_gy = mesh.shape["gx"], mesh.shape["gy"]
    return jax.shard_map(
        functools.partial(per_device, n_gx, n_gy),
        mesh=mesh,
        in_specs=(
            P(None, None, "gx", "gy"),
            P(None, "gx", "gy"),
            P("gx", "gy"),
            P(None, "gx", "gy"),
            P("gx", "gy"),
            P("gx", "gy"),
        ),
        out_specs=P(None, None, "gx", "gy"),
        check_vma=False,
    )
```

```python
import functools

import jax
import jax.numpy as jnp
from jax import lax
from jax.experimental import pallas as pl
from jax.experimental.pallas import tpu as pltpu
from jax.sharding import PartitionSpec as P

TILE = 4
CHUNK = 16
SUBLANES = 8
LANES = 128
lap_weight = 0.25
prior_weight = 0.05
couple_weight = 0.5
step_length = 1.0
epsilon = 1e-06
highest = lax.Precision.HIGHEST
MESH = pl.DeviceIdType.MESH
F32 = jnp.float32
BF16 = jnp.bfloat16


def split(x):
    high = x.astype(BF16)
    return high, (x - high.astype(F32)).astype(BF16)


def dot_nn(a, b, precision=None):
    return lax.dot_general(
        a, b, (((1,), (0,)), ((), ())), precision=precision, preferred_element_type=F32
    )


def dot_nt(a, b, precision=None):
    return lax.dot_general(
        a, b, (((1,), (1,)), ((), ())), precision=precision, preferred_element_type=F32
    )


def total(x):
    return jnp.sum(jnp.sum(x, axis=1, keepdims=True), axis=0, keepdims=True)


def kernel(
    n_gx, n_gy, size,
    state, background, tile, mask, values, variance,
    out,
    fld, hf, xl, xh, yp, yr, dl, dh, hmat, gpart, grecv, gres, gsum, spart, srecv, small,
    send, recv, gsend, grsem, asend, arsem, ssend, srsem,
):
    layers, rows, count, cols = state.shape
    chunks = count // CHUNK
    n_dev = n_gx * n_gy
    gx = lax.axis_index("gx")
    gy = lax.axis_index("gy")
    up = lax.rem(gx + 1, n_gx)
    down = lax.rem(gx + n_gx - 1, n_gx)
    side = lax.rem(gy + 1, n_gy)
    me = gx * n_gy + gy

    def device(offset):
        other = lax.rem(me + offset, n_dev)
        return other, (lax.div(other, n_gy), lax.rem(other, n_gy))

    barrier = pltpu.get_barrier_semaphore()

    def greet(offset, carry):
        pl.semaphore_signal(barrier, inc=1, device_id=device(offset)[1], device_id_type=MESH)
        return carry

    lax.fori_loop(1, n_dev, greet, 0)

    lane = lax.broadcasted_iota(jnp.int32, (CHUNK, LANES), 1)
    lane8 = lax.broadcasted_iota(jnp.int32, (SUBLANES, LANES), 1)
    groups = CHUNK // SUBLANES
    zone = LANES // (layers * rows * groups)
    owner = lax.rem(lax.div(lane8 + zone // 2, zone), LANES // zone)

    def place(l, r, s):
        return (l * rows + r) * groups + s

    def pack(f, c):
        packed = None
        for l in range(layers):
            for r in range(rows):
                for s in range(groups):
                    start = pl.multiple_of(c * CHUNK + s * SUBLANES, SUBLANES)
                    ps = pl.ds(start, SUBLANES)
                    ends = jnp.where(
                        lane8 < LANES // 2,
                        fld[f, l, r, ps, pl.ds(0, LANES)],
                        fld[f, l, r, ps, pl.ds(cols - LANES, LANES)],
                    )
                    k = place(l, r, s)
                    if k == 0:
                        packed = ends
                    else:
                        packed = jnp.where(owner == k, pltpu.roll(ends, k * zone, 1), packed)
        yp[f, c] = packed

    def unpack(packed, l, r):
        shifts = [place(l, r, s) * zone for s in range(groups)]
        return jnp.concatenate(
            [pltpu.roll(packed, LANES - k, 1) if k else packed for k in shifts], axis=0
        )

    def copies(f, c):
        ps = pl.ds(pl.multiple_of(c * CHUNK, CHUNK), CHUNK)
        pairs = (
            (fld.at[f, :, pl.ds(rows - 2, 2), ps, :], xl.at[f, :, :, ps, :], (up, gy)),
            (fld.at[f, :, pl.ds(0, 2), ps, :], xh.at[f, :, :, ps, :], (down, gy)),
            (yp.at[f, c], yr.at[f, c], (gx, side)),
            (yp.at[f, c], dl.at[f, c], (up, side)),
            (yp.at[f, c], dh.at[f, c], (down, side)),
        )
        return [
            pltpu.make_async_remote_copy(
                src_ref=source,
                dst_ref=target,
                send_sem=send.at[f, kind, c],
                recv_sem=recv.at[f, kind, c],
                device_id=where,
                device_id_type=MESH,
            )
            for kind, (source, target, where) in enumerate(pairs)
        ]

    def prior(f, c, emit):
        ps = pl.ds(pl.multiple_of(c * CHUNK, CHUNK), CHUNK)
        below, level, above = dl[f, c], yr[f, c], dh[f, c]
        edges = [
            [unpack(below, l, rows - 1)]
            + [unpack(level, l, r) for r in range(rows)]
            + [unpack(above, l, 0)]
            for l in range(layers)
        ]
        for r in range(rows):
            for l in range(layers):

                def row(k):
                    if k < 0:
                        return xl[f, l, k + 2, ps, :]
                    if k >= rows:
                        return xh[f, l, k - rows, ps, :]
                    return fld[f, l, k, ps, :]

                here = row(r)
                near = row(r - 1) + row(r + 1)
                far = row(r - 2) + row(r + 2)
                wide = 0.125 * near - here
                edge_here = edges[l][r + 1]
                edge_wide = 0.125 * (edges[l][r] + edges[l][r + 2]) - edge_here

                def shifted(x, e, by):
                    left = pltpu.roll(x, by, 1)
                    first = jnp.where(lane < by, pltpu.roll(e, by, 1), left[:, :LANES])
                    left = jnp.concatenate([first, left[:, LANES:]], axis=1)
                    right = pltpu.roll(x, cols - by, 1)
                    last = jnp.where(
                        lane >= LANES - by, pltpu.roll(e, LANES - by, 1), right[:, cols - LANES :]
                    )
                    right = jnp.concatenate([right[:, : cols - LANES], last], axis=1)
                    return left + right

                curved = 4.25 * here - near + 0.0625 * (far + shifted(here, edge_here, 2))
                curved = curved + shifted(wide, edge_wide, 1)
                other = fld[f, 1 - l, r, ps, :]
                emit(l, r, ps, -prior_weight * (curved + couple_weight * (here - other)))

    def begin(c, carry):
        ps = pl.ds(pl.multiple_of(c * CHUNK, CHUNK), CHUNK)
        for l in range(layers):
            for r in range(rows):
                fld[0, l, r, ps, :] = state[l, r, ps, :] - background[l, pl.ds(r, 1), :]
        pack(0, c)
        return carry

    lax.fori_loop(0, chunks, begin, 0)
    pl.semaphore_wait(barrier, n_dev - 1)

    def send_first(c, carry):
        for copy in copies(0, c):
            copy.start()
        return carry

    lax.fori_loop(0, chunks, send_first, 0)

    n_obs = tile.shape[1]
    column = lax.broadcasted_iota(jnp.int32, (cols, n_obs), 0)
    hit = lax.div(column, TILE) == tile[...]
    for r in range(rows):
        weights = 0.25 * mask[pl.ds(r * TILE, TILE), :].astype(F32)
        weights = jnp.concatenate([weights, weights], axis=0)
        weights = jnp.concatenate([weights] * (cols // (2 * TILE)), axis=0)
        hmat[r] = jnp.where(hit, weights, 0.0).astype(BF16)

    def mapped_of(upper):
        acc = jnp.zeros((2 * count, n_obs), F32)
        for r in range(rows):
            acc = acc + dot_nn(jnp.concatenate(split(upper(r)), axis=0), hmat[r])
        return acc[:count] + acc[count:]

    def spread_of(innovation, emit):
        both = jnp.concatenate(split(innovation), axis=0)
        for r in range(rows):
            back = dot_nt(both, hmat[r])
            emit(r, back[:count] + back[count:])

    def put_obs(r, x):
        hf[0, r] = x

    mapped = mapped_of(lambda r: state[0, r])
    spread_of((values[...] - mapped) / variance[...], put_obs)

    def gradient(c, carry):
        for copy in copies(0, c):
            copy.wait_recv()

        def emit(l, r, ps, x):
            fld[1, l, r, ps, :] = x + hf[0, r, ps, :] if l == 0 else x

        prior(0, c, emit)
        pack(1, c)
        for copy in copies(1, c):
            copy.start()
        return carry

    lax.fori_loop(0, chunks, gradient, 0)

    same = jnp.zeros((2 * count, 2 * count), F32)
    cross = jnp.zeros((2 * count, 2 * count), F32)
    for l in range(layers):
        for r in range(rows):
            high, low = split(jnp.concatenate([fld[0, l, r], fld[1, l, r]], axis=0))
            same = same + dot_nt(high, high)
            cross = cross + dot_nt(high, low)
    gram = same + cross + cross.T
    share = gpart.shape[1]
    owners = 2 * count // share
    for o in range(owners):
        gpart[o] = gram[o * share : (o + 1) * share]
    if owners < n_dev:
        gpart[pl.ds(owners, n_dev - owners)] = jnp.zeros((n_dev - owners, share, 2 * count), F32)

    def scatter(k):
        other, where = device(k)
        return pltpu.make_async_remote_copy(
            src_ref=gpart.at[other], dst_ref=grecv.at[k], send_sem=gsend.at[k],
            recv_sem=grsem.at[k], device_id=where, device_id_type=MESH,
        )

    def gather(k):
        other, where = device(k)
        return pltpu.make_async_remote_copy(
            src_ref=gsum, dst_ref=gres.at[me], send_sem=asend.at[k],
            recv_sem=arsem.at[k], device_id=where, device_id_type=MESH,
        )

    def share_out(k):
        other, where = device(k)
        return pltpu.make_async_remote_copy(
            src_ref=spart, dst_ref=srecv.at[k], send_sem=ssend.at[k],
            recv_sem=srsem.at[k], device_id=where, device_id_type=MESH,
        )

    def each(make, act):
        def step(k, carry):
            act(make(k))
            return carry

        lax.fori_loop(1, n_dev, step, 0)

    each(scatter, lambda copy: copy.start())

    mapped = mapped_of(lambda r: fld[1, 0, r])
    spread_of(-mapped / variance[...], put_obs)

    def second(c, carry):
        for copy in copies(1, c):
            copy.wait_recv()

        def emit(l, r, ps, x):
            hf[l, r, ps, :] = x + hf[0, r, ps, :] if l == 0 else x

        prior(1, c, emit)
        return carry

    half = chunks // 2
    lax.fori_loop(0, half, second, 0)
    grecv[0] = gpart[me]
    each(scatter, lambda copy: copy.wait_recv())
    gsum[...] = jnp.sum(grecv[...], axis=0)
    gres[me] = gsum[...]
    each(gather, lambda copy: copy.start())
    lax.fori_loop(half, chunks, second, 0)

    each(gather, lambda copy: copy.wait_recv())
    gram = jnp.concatenate([gres[o] for o in range(owners)], axis=0)
    eye = (
        lax.broadcasted_iota(jnp.int32, (count, count), 0)
        == lax.broadcasted_iota(jnp.int32, (count, count), 1)
    ).astype(F32)

    def mixing(matrix):
        diagonal = matrix * eye
        distance = (
            jnp.sum(diagonal, axis=1, keepdims=True)
            + jnp.sum(diagonal, axis=0, keepdims=True)
            - 2.0 * matrix
        )
        width = total(distance * (1.0 - eye)) / (count * (count - 1.0) * size) + epsilon
        weight = jnp.exp(-distance / (2.0 * width * size))
        pull = (jnp.sum(weight, axis=1, keepdims=True) * eye - weight) / (width * count)
        return weight / count, pull

    dev_gram = gram[:count, :count]
    attract, pull = mixing(dev_gram)
    small[0] = jnp.concatenate([pull, attract], axis=1)
    weights = small[0]
    small[1] = dot_nn(weights, gram, highest)
    partial = small[1]
    square = dot_nt(partial, weights, highest)
    crossed = dot_nt(gram[:count], weights, highest)
    small[2] = jnp.concatenate([square, crossed], axis=1)
    square = small[2, :, pl.ds(0, count)]
    crossed = small[2, :, pl.ds(count, count)]
    scale = step_length / jnp.sqrt(total(square * eye) / (count * size) + epsilon)
    next_gram = dev_gram + scale * (crossed + partial[:, :count]) + scale * scale * square
    attract_next, pull_next = mixing(next_gram)
    products = scale * dot_nn(jnp.concatenate([attract_next, pull_next], axis=0), weights, highest)
    on_dev = pull_next + products[count:, :count]
    on_grad = attract_next + products[:count, :count] + products[count:, count:]
    on_second = products[:count, count:]
    def mix(parts, fields, emit):
        high, low = split(jnp.concatenate(parts, axis=1))
        both = jnp.concatenate([high, low], axis=0)
        for l in range(layers):
            for r in range(rows):
                top, rest = split(jnp.concatenate(fields(l, r), axis=0))
                main = dot_nn(both, top)
                emit(l, r, main[:count] + main[count:] + dot_nn(high, rest))

    sums = [jnp.zeros((count, cols), F32)]

    def put_drift(l, r, x):
        hf[l, r] = x
        sums[0] = sums[0] + x * x

    def put_middle(l, r, x):
        out[l, r] = state[l, r] + scale * x

    mix(
        [on_dev, on_grad, on_second],
        lambda l, r: [fld[0, l, r], fld[1, l, r], hf[l, r]],
        put_drift,
    )
    sums = sums[0]
    sums = jnp.sum(sums, axis=0, keepdims=True)
    folded = sums[:, :LANES]
    for k in range(1, cols // LANES):
        folded = folded + sums[:, k * LANES : (k + 1) * LANES]
    spart[...] = folded
    srecv[0] = folded
    each(share_out, lambda copy: copy.start())
    mix([pull, attract], lambda l, r: [fld[0, l, r], fld[1, l, r]], put_middle)
    each(share_out, lambda copy: copy.wait_recv())
    whole = total(jnp.sum(srecv[...], axis=0))
    scale_next = step_length / jnp.sqrt(whole / (count * size) + epsilon)
    for l in range(layers):
        for r in range(rows):
            out[l, r] = out[l, r] + scale_next * hf[l, r]

    def drain(c, carry):
        for f in range(2):
            for copy in copies(f, c):
                copy.wait_send()
        return carry

    lax.fori_loop(0, chunks, drain, 0)
    each(scatter, lambda copy: copy.wait_send())
    each(gather, lambda copy: copy.wait_send())
    each(share_out, lambda copy: copy.wait_send())


def per_device(n_gx, n_gy, particles, background, obs_tile, obs_mask, obs_value, obs_var):
    count, layers, rows, cols = particles.shape
    assert rows == TILE and n_gy == 2 and count % CHUNK == 0
    n_dev = n_gx * n_gy
    size = float(layers * rows * cols * n_dev)
    n_obs = obs_tile.shape[1]
    share = max(1, 2 * count // n_dev)
    chunks = count // CHUNK
    dma = pltpu.SemaphoreType.DMA
    planes = particles.transpose(1, 2, 0, 3)
    vmem = pl.BlockSpec(memory_space=pltpu.VMEM)
    result = pl.pallas_call(
        functools.partial(kernel, n_gx, n_gy, size),
        out_shape=jax.ShapeDtypeStruct((layers, rows, count, cols), F32),
        in_specs=[vmem] * 6,
        out_specs=vmem,
        scratch_shapes=[
            pltpu.VMEM((2, layers, rows, count, cols), F32),
            pltpu.VMEM((layers, rows, count, cols), F32),
            pltpu.VMEM((2, layers, 2, count, cols), F32),
            pltpu.VMEM((2, layers, 2, count, cols), F32),
            pltpu.VMEM((2, chunks, SUBLANES, LANES), F32),
            pltpu.VMEM((2, chunks, SUBLANES, LANES), F32),
            pltpu.VMEM((2, chunks, SUBLANES, LANES), F32),
            pltpu.VMEM((2, chunks, SUBLANES, LANES), F32),
            pltpu.VMEM((rows, cols, n_obs), BF16),
            pltpu.VMEM((n_dev, share, 2 * count), F32),
            pltpu.VMEM((n_dev, share, 2 * count), F32),
            pltpu.VMEM((n_dev, share, 2 * count), F32),
            pltpu.VMEM((share, 2 * count), F32),
            pltpu.VMEM((1, LANES), F32),
            pltpu.VMEM((n_dev, 1, LANES), F32),
            pltpu.VMEM((3, count, 2 * count), F32),
            dma((2, 5, chunks)),
            dma((2, 5, chunks)),
        ]
        + [dma((n_dev,))] * 6,
        compiler_params=pltpu.CompilerParams(
            collective_id=0, has_side_effects=True, vmem_limit_bytes=48 * 2**20
        ),
    )(planes, background, obs_tile, obs_mask[:, 0], obs_value, obs_var)
    return result.transpose(2, 0, 1, 3)


def solution(mesh):
    n_gx, n_gy = mesh.shape["gx"], mesh.shape["gy"]
    return jax.shard_map(
        functools.partial(per_device, n_gx, n_gy),
        mesh=mesh,
        in_specs=(
            P(None, None, "gx", "gy"),
            P(None, "gx", "gy"),
            P("gx", "gy"),
            P(None, "gx", "gy"),
            P("gx", "gy"),
            P("gx", "gy"),
        ),
        out_specs=P(None, None, "gx", "gy"),
        check_vma=False,
    )
```

```python
import functools

import jax
import jax.numpy as jnp
from jax import lax
from jax.experimental import pallas as pl
from jax.experimental.pallas import tpu as pltpu
from jax.sharding import PartitionSpec as P

TILE = 4
CHUNK = 16
SUBLANES = 8
LANES = 128
lap_weight = 0.25
prior_weight = 0.05
couple_weight = 0.5
step_length = 1.0
epsilon = 1e-06
highest = lax.Precision.HIGHEST
MESH = pl.DeviceIdType.MESH
F32 = jnp.float32
BF16 = jnp.bfloat16


def split(x):
    high = x.astype(BF16)
    return high, (x - high.astype(F32)).astype(BF16)


def dot_nn(a, b, precision=None):
    return lax.dot_general(
        a, b, (((1,), (0,)), ((), ())), precision=precision, preferred_element_type=F32
    )


def dot_nt(a, b, precision=None):
    return lax.dot_general(
        a, b, (((1,), (1,)), ((), ())), precision=precision, preferred_element_type=F32
    )


def dot_split(a, b, dot):
    high, low = split(a)
    top, rest = split(b)
    main = dot(jnp.concatenate([high, low], axis=0), top)
    return main[: a.shape[0]] + main[a.shape[0] :] + dot(high, rest)


def total(x):
    return jnp.sum(jnp.sum(x, axis=1, keepdims=True), axis=0, keepdims=True)


def kernel(
    n_gx, n_gy, size,
    state, background, tile, mask, values, variance,
    out,
    fld, hf, xl, xh, yp, yr, dl, dh, hmat, gpart, grecv, gres, gsum, spart, srecv, small,
    send, recv, gsend, grsem, asend, arsem, ssend, srsem,
):
    layers, rows, count, cols = state.shape
    chunks = count // CHUNK
    n_dev = n_gx * n_gy
    gx = lax.axis_index("gx")
    gy = lax.axis_index("gy")
    up = lax.rem(gx + 1, n_gx)
    down = lax.rem(gx + n_gx - 1, n_gx)
    side = lax.rem(gy + 1, n_gy)
    me = gx * n_gy + gy

    def device(offset):
        other = lax.rem(me + offset, n_dev)
        return other, (lax.div(other, n_gy), lax.rem(other, n_gy))

    barrier = pltpu.get_barrier_semaphore()

    def greet(offset, carry):
        pl.semaphore_signal(barrier, inc=1, device_id=device(offset)[1], device_id_type=MESH)
        return carry

    lax.fori_loop(1, n_dev, greet, 0)

    lane = lax.broadcasted_iota(jnp.int32, (CHUNK, LANES), 1)
    lane8 = lax.broadcasted_iota(jnp.int32, (SUBLANES, LANES), 1)
    groups = CHUNK // SUBLANES
    zone = LANES // (layers * rows * groups)
    owner = lax.rem(lax.div(lane8 + zone // 2, zone), LANES // zone)

    def place(l, r, s):
        return (l * rows + r) * groups + s

    def pack(f, c):
        packed = None
        for l in range(layers):
            for r in range(rows):
                for s in range(groups):
                    start = pl.multiple_of(c * CHUNK + s * SUBLANES, SUBLANES)
                    ps = pl.ds(start, SUBLANES)
                    ends = jnp.where(
                        lane8 < LANES // 2,
                        fld[f, l, r, ps, pl.ds(0, LANES)],
                        fld[f, l, r, ps, pl.ds(cols - LANES, LANES)],
                    )
                    k = place(l, r, s)
                    if k == 0:
                        packed = ends
                    else:
                        packed = jnp.where(owner == k, pltpu.roll(ends, k * zone, 1), packed)
        yp[f, c] = packed

    def unpack(packed, l, r):
        shifts = [place(l, r, s) * zone for s in range(groups)]
        return jnp.concatenate(
            [pltpu.roll(packed, LANES - k, 1) if k else packed for k in shifts], axis=0
        )

    def copies(f, c):
        ps = pl.ds(pl.multiple_of(c * CHUNK, CHUNK), CHUNK)
        pairs = (
            (fld.at[f, :, pl.ds(rows - 2, 2), ps, :], xl.at[f, :, :, ps, :], (up, gy)),
            (fld.at[f, :, pl.ds(0, 2), ps, :], xh.at[f, :, :, ps, :], (down, gy)),
            (yp.at[f, c], yr.at[f, c], (gx, side)),
            (yp.at[f, c], dl.at[f, c], (up, side)),
            (yp.at[f, c], dh.at[f, c], (down, side)),
        )
        return [
            pltpu.make_async_remote_copy(
                src_ref=source,
                dst_ref=target,
                send_sem=send.at[f, kind, c],
                recv_sem=recv.at[f, kind, c],
                device_id=where,
                device_id_type=MESH,
            )
            for kind, (source, target, where) in enumerate(pairs)
        ]

    def prior(f, c, emit):
        ps = pl.ds(pl.multiple_of(c * CHUNK, CHUNK), CHUNK)
        below, level, above = dl[f, c], yr[f, c], dh[f, c]
        edges = [
            [unpack(below, l, rows - 1)]
            + [unpack(level, l, r) for r in range(rows)]
            + [unpack(above, l, 0)]
            for l in range(layers)
        ]
        for r in range(rows):
            for l in range(layers):

                def row(k):
                    if k < 0:
                        return xl[f, l, k + 2, ps, :]
                    if k >= rows:
                        return xh[f, l, k - rows, ps, :]
                    return fld[f, l, k, ps, :]

                here = row(r)
                near = row(r - 1) + row(r + 1)
                far = row(r - 2) + row(r + 2)
                wide = 0.125 * near - here
                edge_here = edges[l][r + 1]
                edge_wide = 0.125 * (edges[l][r] + edges[l][r + 2]) - edge_here

                def shifted(x, e, by):
                    left = pltpu.roll(x, by, 1)
                    first = jnp.where(lane < by, pltpu.roll(e, by, 1), left[:, :LANES])
                    left = jnp.concatenate([first, left[:, LANES:]], axis=1)
                    right = pltpu.roll(x, cols - by, 1)
                    last = jnp.where(
                        lane >= LANES - by, pltpu.roll(e, LANES - by, 1), right[:, cols - LANES :]
                    )
                    right = jnp.concatenate([right[:, : cols - LANES], last], axis=1)
                    return left + right

                curved = 4.25 * here - near + 0.0625 * (far + shifted(here, edge_here, 2))
                curved = curved + shifted(wide, edge_wide, 1)
                other = fld[f, 1 - l, r, ps, :]
                emit(l, r, ps, -prior_weight * (curved + couple_weight * (here - other)))

    def begin(c, carry):
        ps = pl.ds(pl.multiple_of(c * CHUNK, CHUNK), CHUNK)
        for l in range(layers):
            for r in range(rows):
                fld[0, l, r, ps, :] = state[l, r, ps, :] - background[l, pl.ds(r, 1), :]
        pack(0, c)
        return carry

    lax.fori_loop(0, chunks, begin, 0)
    pl.semaphore_wait(barrier, n_dev - 1)

    def send_first(c, carry):
        for copy in copies(0, c):
            copy.start()
        return carry

    lax.fori_loop(0, chunks, send_first, 0)

    n_obs = tile.shape[1]
    column = lax.broadcasted_iota(jnp.int32, (cols, n_obs), 0)
    hit = lax.div(column, TILE) == tile[...]
    for r in range(rows):
        weights = 0.25 * mask[pl.ds(r * TILE, TILE), :].astype(F32)
        weights = jnp.concatenate([weights, weights], axis=0)
        weights = jnp.concatenate([weights] * (cols // (2 * TILE)), axis=0)
        hmat[r] = jnp.where(hit, weights, 0.0).astype(BF16)

    def mapped_of(upper):
        acc = jnp.zeros((2 * count, n_obs), F32)
        for r in range(rows):
            acc = acc + dot_nn(jnp.concatenate(split(upper(r)), axis=0), hmat[r])
        return acc[:count] + acc[count:]

    def spread_of(innovation, emit):
        both = jnp.concatenate(split(innovation), axis=0)
        for r in range(rows):
            back = dot_nt(both, hmat[r])
            emit(r, back[:count] + back[count:])

    def put_obs(r, x):
        hf[0, r] = x

    mapped = mapped_of(lambda r: state[0, r])
    spread_of((values[...] - mapped) / variance[...], put_obs)

    def gradient(c, carry):
        for copy in copies(0, c):
            copy.wait_recv()

        def emit(l, r, ps, x):
            fld[1, l, r, ps, :] = x + hf[0, r, ps, :] if l == 0 else x

        prior(0, c, emit)
        pack(1, c)
        return carry

    def send_second(c, carry):
        for copy in copies(1, c):
            copy.start()
        return carry

    def both(c, carry):
        gradient(c, carry)
        return send_second(c, carry)

    lax.fori_loop(0, chunks // 2, both, 0)
    lax.fori_loop(chunks // 2, chunks, gradient, 0)

    same = jnp.zeros((2 * count, 2 * count), F32)
    cross = jnp.zeros((2 * count, 2 * count), F32)
    for l in range(layers):
        for r in range(rows):
            high, low = split(jnp.concatenate([fld[0, l, r], fld[1, l, r]], axis=0))
            same = same + dot_nt(high, high)
            cross = cross + dot_nt(high, low)
    gram = same + cross + cross.T
    share = gpart.shape[1]
    owners = 2 * count // share
    for o in range(owners):
        gpart[o] = gram[o * share : (o + 1) * share]
    if owners < n_dev:
        gpart[pl.ds(owners, n_dev - owners)] = jnp.zeros((n_dev - owners, share, 2 * count), F32)

    def scatter(k):
        other, where = device(k)
        return pltpu.make_async_remote_copy(
            src_ref=gpart.at[other], dst_ref=grecv.at[k], send_sem=gsend.at[k],
            recv_sem=grsem.at[k], device_id=where, device_id_type=MESH,
        )

    def gather(k):
        other, where = device(k)
        return pltpu.make_async_remote_copy(
            src_ref=gsum, dst_ref=gres.at[me], send_sem=asend.at[k],
            recv_sem=arsem.at[k], device_id=where, device_id_type=MESH,
        )

    def share_out(k):
        other, where = device(k)
        return pltpu.make_async_remote_copy(
            src_ref=spart, dst_ref=srecv.at[k], send_sem=ssend.at[k],
            recv_sem=srsem.at[k], device_id=where, device_id_type=MESH,
        )

    def each(make, act):
        def step(k, carry):
            act(make(k))
            return carry

        lax.fori_loop(1, n_dev, step, 0)

    each(scatter, lambda copy: copy.start())
    lax.fori_loop(chunks // 2, chunks, send_second, 0)

    mapped = mapped_of(lambda r: fld[1, 0, r])
    spread_of(-mapped / variance[...], put_obs)

    def second(c, carry):
        for copy in copies(1, c):
            copy.wait_recv()

        def emit(l, r, ps, x):
            hf[l, r, ps, :] = x + hf[0, r, ps, :] if l == 0 else x

        prior(1, c, emit)
        return carry

    half = 0
    lax.fori_loop(0, half, second, 0)
    grecv[0] = gpart[me]
    each(scatter, lambda copy: copy.wait_recv())
    gsum[...] = jnp.sum(grecv[...], axis=0)
    gres[me] = gsum[...]
    each(gather, lambda copy: copy.start())
    lax.fori_loop(half, chunks, second, 0)

    each(gather, lambda copy: copy.wait_recv())
    gram = jnp.concatenate([gres[o] for o in range(owners)], axis=0)
    eye = (
        lax.broadcasted_iota(jnp.int32, (count, count), 0)
        == lax.broadcasted_iota(jnp.int32, (count, count), 1)
    ).astype(F32)

    def mixing(matrix):
        diagonal = matrix * eye
        distance = (
            jnp.sum(diagonal, axis=1, keepdims=True)
            + jnp.sum(diagonal, axis=0, keepdims=True)
            - 2.0 * matrix
        )
        width = total(distance * (1.0 - eye)) / (count * (count - 1.0) * size) + epsilon
        weight = jnp.exp(-distance / (2.0 * width * size))
        pull = (jnp.sum(weight, axis=1, keepdims=True) * eye - weight) / (width * count)
        return weight / count, pull

    dev_gram = gram[:count, :count]
    attract, pull = mixing(dev_gram)
    small[0] = jnp.concatenate([pull, attract], axis=1)
    weights = small[0]
    small[1] = dot_split(weights, gram, dot_nn)
    partial = small[1]
    square = dot_split(partial, weights, dot_nt)
    crossed = dot_split(gram[:count], weights, dot_nt)
    small[2] = jnp.concatenate([square, crossed], axis=1)
    square = small[2, :, pl.ds(0, count)]
    crossed = small[2, :, pl.ds(count, count)]
    scale = step_length / jnp.sqrt(total(square * eye) / (count * size) + epsilon)
    next_gram = dev_gram + scale * (crossed + partial[:, :count]) + scale * scale * square
    attract_next, pull_next = mixing(next_gram)
    products = scale * dot_split(
        jnp.concatenate([attract_next, pull_next], axis=0), weights, dot_nn
    )
    on_dev = pull_next + products[count:, :count]
    on_grad = attract_next + products[:count, :count] + products[count:, count:]
    on_second = products[:count, count:]
    def mix(parts, fields, emit):
        high, low = split(jnp.concatenate(parts, axis=1))
        both = jnp.concatenate([high, low], axis=0)
        for l in range(layers):
            for r in range(rows):
                top, rest = split(jnp.concatenate(fields(l, r), axis=0))
                main = dot_nn(both, top)
                emit(l, r, main[:count] + main[count:] + dot_nn(high, rest))

    sums = [jnp.zeros((count, cols), F32)]

    def put_drift(l, r, x):
        hf[l, r] = x
        sums[0] = sums[0] + x * x

    def put_middle(l, r, x):
        out[l, r] = state[l, r] + scale * x

    mix(
        [on_dev, on_grad, on_second],
        lambda l, r: [fld[0, l, r], fld[1, l, r], hf[l, r]],
        put_drift,
    )
    sums = sums[0]
    sums = jnp.sum(sums, axis=0, keepdims=True)
    folded = sums[:, :LANES]
    for k in range(1, cols // LANES):
        folded = folded + sums[:, k * LANES : (k + 1) * LANES]
    spart[...] = folded
    srecv[0] = folded
    each(share_out, lambda copy: copy.start())
    mix([pull, attract], lambda l, r: [fld[0, l, r], fld[1, l, r]], put_middle)
    each(share_out, lambda copy: copy.wait_recv())
    whole = total(jnp.sum(srecv[...], axis=0))
    scale_next = step_length / jnp.sqrt(whole / (count * size) + epsilon)
    for l in range(layers):
        for r in range(rows):
            out[l, r] = out[l, r] + scale_next * hf[l, r]

    def drain(c, carry):
        for f in range(2):
            for copy in copies(f, c):
                copy.wait_send()
        return carry

    lax.fori_loop(0, chunks, drain, 0)
    each(scatter, lambda copy: copy.wait_send())
    each(gather, lambda copy: copy.wait_send())
    each(share_out, lambda copy: copy.wait_send())


def per_device(n_gx, n_gy, particles, background, obs_tile, obs_mask, obs_value, obs_var):
    count, layers, rows, cols = particles.shape
    assert rows == TILE and n_gy == 2 and count % CHUNK == 0
    n_dev = n_gx * n_gy
    size = float(layers * rows * cols * n_dev)
    n_obs = obs_tile.shape[1]
    share = max(1, 2 * count // n_dev)
    chunks = count // CHUNK
    dma = pltpu.SemaphoreType.DMA
    planes = particles.transpose(1, 2, 0, 3)
    vmem = pl.BlockSpec(memory_space=pltpu.VMEM)
    result = pl.pallas_call(
        functools.partial(kernel, n_gx, n_gy, size),
        out_shape=jax.ShapeDtypeStruct((layers, rows, count, cols), F32),
        in_specs=[vmem] * 6,
        out_specs=vmem,
        scratch_shapes=[
            pltpu.VMEM((2, layers, rows, count, cols), F32),
            pltpu.VMEM((layers, rows, count, cols), F32),
            pltpu.VMEM((2, layers, 2, count, cols), F32),
            pltpu.VMEM((2, layers, 2, count, cols), F32),
            pltpu.VMEM((2, chunks, SUBLANES, LANES), F32),
            pltpu.VMEM((2, chunks, SUBLANES, LANES), F32),
            pltpu.VMEM((2, chunks, SUBLANES, LANES), F32),
            pltpu.VMEM((2, chunks, SUBLANES, LANES), F32),
            pltpu.VMEM((rows, cols, n_obs), BF16),
            pltpu.VMEM((n_dev, share, 2 * count), F32),
            pltpu.VMEM((n_dev, share, 2 * count), F32),
            pltpu.VMEM((n_dev, share, 2 * count), F32),
            pltpu.VMEM((share, 2 * count), F32),
            pltpu.VMEM((1, LANES), F32),
            pltpu.VMEM((n_dev, 1, LANES), F32),
            pltpu.VMEM((3, count, 2 * count), F32),
            dma((2, 5, chunks)),
            dma((2, 5, chunks)),
        ]
        + [dma((n_dev,))] * 6,
        compiler_params=pltpu.CompilerParams(
            collective_id=0, has_side_effects=True, vmem_limit_bytes=48 * 2**20
        ),
    )(planes, background, obs_tile, obs_mask[:, 0], obs_value, obs_var)
    return result.transpose(2, 0, 1, 3)


def solution(mesh):
    n_gx, n_gy = mesh.shape["gx"], mesh.shape["gy"]
    return jax.shard_map(
        functools.partial(per_device, n_gx, n_gy),
        mesh=mesh,
        in_specs=(
            P(None, None, "gx", "gy"),
            P(None, "gx", "gy"),
            P("gx", "gy"),
            P(None, "gx", "gy"),
            P("gx", "gy"),
            P("gx", "gy"),
        ),
        out_specs=P(None, None, "gx", "gy"),
        check_vma=False,
    )
```
